256 devices in a mesh: row: 32 (over x_hi, z, core), col: 8 (over y, x_lo).
Axes of the slice: x: 4 (x_hi: 2, x_lo: 2; x = x_hi * 2 + x_lo), y: 4, z: 8, core: 2. Of those that a mesh axis runs over, the one named last changes fastest.
Arguments:
- p_tiles: bfloat16 [1024, 2, 128, 128], P(('row', 'col')), may hold values from -0.5 to 0.5
- p_cols: int32 [1024, 2], P(('row', 'col')), may hold values from 0 to 31, as said below
- q_tiles: bfloat16 [1024, 6, 128, 128], P(('row', 'col')), may hold values from -1.796875 to 1.796875
- q_cols: int32 [1024, 6], P(('row', 'col')), may hold values from 0 to 31, all different within a row
Outputs:
- coarse: float32 [4096, 4096], P('row', 'col')
The draws below stay inside these ranges and needn't reach their ends.
Inputs may be any that keep to these rules, and one draw needn't show every extreme that they name: `p_cols`: the 2 coarse tiles in one row differ; among the fine blocks held by the devices of one index of col, every coarse tile is named at least once and at most 16 times, and some tile exactly 16 times. `q_cols`: the 6 coarse tiles in one row differ; every coarse tile appears somewhere.
All inputs are finite; a program needn't handle non-finite values.
Results may differ from the reference program's by a relative error of at most 0.0003.
Values may be sent and summed in bfloat16 or wider, within the bound.
A program may use at most 128 MiB of HBM per device.

```python
import math
import jax
import jax.numpy as jnp
from jax import lax

BT = 128
FT_DEV = 4
KP = 2
KQ = 6
CT = 32
NFT = 1024


def draw_p_cols(key, part):
    groups = NFT // (FT_DEV * CT)
    quarter = CT // 4
    mean_load = FT_DEV * KP
    profile = jnp.concatenate([jnp.full((quarter,), 2 * mean_load, jnp.int32), jnp.full((quarter,), mean_load, jnp.int32), jnp.full((CT - 2 * quarter,), mean_load // 2, jnp.int32)])
    bounds = jnp.cumsum(profile)
    total = CT * mean_load
    half_len = total // 2

    def one_group(group_key):
        labels = jax.random.permutation(jax.random.fold_in(group_key, 1), CT).astype(jnp.int32)
        position = jnp.arange(total, dtype=jnp.int32)
        which = jnp.sum((position[:, None] >= bounds[None, :]).astype(jnp.int32), axis=1)
        listing = jnp.take(labels, which)
        paired = jnp.stack([listing[:half_len], listing[half_len:]], axis=1)
        order = jax.random.permutation(jax.random.fold_in(group_key, 2), half_len)
        return jnp.take(paired, order, axis=0)
    keys = jax.vmap(lambda index: jax.random.fold_in(key, index))(jnp.arange(groups, dtype=jnp.int32))
    stacked = jax.vmap(one_group)(keys)
    shaped = stacked.reshape(groups, CT, FT_DEV, KP)
    return jnp.transpose(shaped, (1, 0, 2, 3)).reshape(NFT, KP).astype(jnp.int32)


def level_of(key, shape, shards, least, high):
    loudness, own = 1.0, jax.random.fold_in(key, 6)
    for dim, parts in shards:
        steps = jnp.exp(jax.random.uniform(jax.random.fold_in(own, dim), (parts,), jnp.float32, least / len(shards), high / len(shards)))
        loudness = loudness * jnp.repeat(steps, shape[dim] // parts).reshape([-1 if axis == dim else 1 for axis in range(len(shape))])
    return loudness


def choose_distinct(stream_key, rows, amount, top, lift):
    order = jax.random.permutation(jax.random.fold_in(stream_key, 1), amount)
    boost = order
    for power in range(3):
        boost = boost * boost // amount
    boost = boost * lift // amount
    chance = jax.random.randint(jax.random.fold_in(stream_key, 2), (rows, amount), 0, 4096) + boost
    sure = jax.random.permutation(jax.random.fold_in(stream_key, 3), rows)[jnp.arange(amount) % rows]
    chance = jnp.where(jnp.arange(rows)[:, None] == sure[None, :], 1 << 14, chance)
    priority = chance * amount + jnp.arange(amount)
    return lax.top_k(priority.astype(jnp.int32), top)[1].astype(jnp.int32)


def normal_values(key, shape, scale, most, cuts=(), kind=jnp.bfloat16):
    loudness = level_of(key, shape, cuts, -0.22, 0.18) if cuts else 1.0
    entries = jax.random.normal(key, shape, jnp.float32) * scale * loudness
    return jnp.minimum(jnp.maximum(entries, -most), most).astype(kind)


def setup_inputs(seed: int = 0) -> dict:
    seeds = jax.random.split(jax.random.key(seed), 5)
    return {
        "p_tiles": normal_values(seeds[0], (NFT, KP, BT, BT), BT ** -0.5, 0.5, ((0, 256),)),
        "p_cols": draw_p_cols(jax.random.fold_in(seeds[4], 71), 0),
        "q_tiles": normal_values(seeds[2], (NFT, KQ, BT, BT), 0.3, 1.796875, ((0, 256),)),
        "q_cols": choose_distinct(seeds[3], NFT, CT, KQ, 1536),
    }


def reference(p_tiles, p_cols, q_tiles, q_cols):
    blocks, per_block, extent, _ = p_tiles.shape
    others = q_tiles.shape[1]
    bundle = math.gcd(blocks, 32)
    count = blocks // bundle
    p_groups = p_tiles.reshape(count, bundle, per_block, extent, extent)
    q_groups = q_tiles.reshape(count, bundle, others, extent, extent)
    p_idgroups = p_cols.reshape(count, bundle, per_block)
    q_idgroups = q_cols.reshape(count, bundle, others)

    def one_bundle(running, inputs):
        p_set, q_set, p_ids, q_ids = inputs
        terms = jnp.einsum("fkab,flad->fklbd", p_set.astype(jnp.float32), q_set.astype(jnp.float32),
                           precision=lax.Precision.HIGHEST)
        row_ids = jnp.broadcast_to(p_ids[:, :, None], (bundle, per_block, others)).astype(jnp.int32)
        col_ids = jnp.broadcast_to(q_ids[:, None, :], (bundle, per_block, others)).astype(jnp.int32)
        running = running.at[row_ids, :, col_ids, :].add(terms)
        return running, None

    start_sum = jnp.zeros((CT, extent, CT, extent), jnp.float32)
    summed, _ = lax.scan(one_bundle, start_sum, (p_groups, q_groups, p_idgroups, q_idgroups))
    return summed.reshape(CT * extent, CT * extent)
```

```python
import functools

import jax
import jax.numpy as jnp
from jax import lax
from jax.experimental import pallas as pl
from jax.experimental.pallas import tpu as pltpu
from jax.sharding import PartitionSpec as P

MESH = pl.DeviceIdType.MESH
BF16, F32 = jnp.bfloat16, jnp.float32
ANY = pl.BlockSpec(memory_space=pl.ANY)
VMEM = pl.BlockSpec(memory_space=pltpu.VMEM)
SMEM = pl.BlockSpec(memory_space=pltpu.SMEM)
RECORD = 640


def place():
    row, col = lax.axis_index("row"), lax.axis_index("col")
    core, z = lax.rem(row, 2), lax.rem(lax.div(row, 2), 8)
    x = lax.div(row, 16) * 2 + lax.rem(col, 2)
    return x, lax.div(col, 2), z, core


def device(x, y, z, core):
    return (lax.div(x, 2) * 16 + z * 2 + core, y * 2 + lax.rem(x, 2))


def shift(v, by, n):
    return lax.rem(v + (by + n), n)


def remote(src, dst, send, recv, where):
    return pltpu.make_async_remote_copy(
        src_ref=src, dst_ref=dst, send_sem=send, recv_sem=recv, device_id=where, device_id_type=MESH
    )


def greet(partners):
    barrier = pltpu.get_barrier_semaphore()
    for partner in partners:
        pl.semaphore_signal(barrier, inc=1, device_id=partner, device_id_type=MESH)
    pl.semaphore_wait(barrier, len(partners))


def gather_kernel(p_ref, q_ref, id_ref, gy, gx, iy, ix, stage, send, recv, local, id_send, id_recv):
    x, y, z, core = place()
    other = 1 - core
    rings = (y, x)

    def member(c, pos, who):
        return device(x, pos, z, who) if c == 0 else device(pos, y, z, who)

    others = [(by, flip) for by in range(4) for flip in range(2) if by or flip]
    partners = [member(0, shift(y, by, 4), other if flip else core) for by, flip in others]
    partners += [member(1, shift(x, by, 4), other if flip else core) for by, flip in others if by]
    greet(partners)

    started = []

    def launch(copy):
        copy.start()
        started.append(copy)

    kept = []

    def stage_block(f):
        for c in range(2):
            for k in range(2):
                stage[c, f, k * 128 : (k + 1) * 128, :] = p_ref[f, k]
        for l in range(6):
            flipped = q_ref[f, l].T
            for c in range(2):
                stage[c, f, 256 + l * 64 : 320 + l * 64, :] = flipped[c * 64 : c * 64 + 64]

    def slot(c, pos, who, h):
        return (gy, gx)[c].at[pos, who, pl.ds(h * 2, 2)]

    def own(c, i, h, pos, who):
        launch(
            remote(
                stage.at[c, pl.ds(h * 2, 2)],
                slot(c, rings[c], core, h),
                send.at[c, i],
                recv.at[c, i],
                member(c, pos, who),
            )
        )

    def forward(c, i, h, src, pos, who):
        launch(
            remote(slot(c, src, core, h), slot(c, src, core, h), send.at[c, i], recv.at[c, i], member(c, pos, who))
        )

    def arrived(c, i, h, src, who):
        ref = slot(c, src, who, h)
        remote(ref, ref, send.at[c, i], recv.at[c, i], member(c, rings[c], other)).wait_recv()

    left = [shift(v, -1, 4) for v in rings]
    right = [shift(v, 1, 4) for v in rings]
    far = [shift(v, 2, 4) for v in rings]
    for f in range(2):
        stage_block(f)
    for c in range(2):
        own(c, 0, 0, right[c], core)
        own(c, 6, 0, rings[c], other)
    for f in range(2, 4):
        stage_block(f)
    for c in range(2):
        own(c, 3, 1, left[c], core)
        own(c, 1, 1, right[c], core)
        own(c, 2, 0, left[c], core)
        own(c, 7, 1, rings[c], other)
    for c in range(2):
        copy = pltpu.make_async_copy(stage.at[c], (gy, gx)[c].at[rings[c], core], local.at[c])
        copy.start()
        kept.append(copy)
        ids = (iy, ix)[c]
        copy = pltpu.make_async_copy(id_ref, ids.at[rings[c], core], local.at[2 + c])
        copy.start()
        kept.append(copy)
        for n, (by, flip) in enumerate(others):
            launch(
                remote(
                    id_ref,
                    ids.at[rings[c], core],
                    id_send.at[c, n],
                    id_recv.at[c, n],
                    member(c, shift(rings[c], by, 4), other if flip else core),
                )
            )
    for c in range(2):
        arrived(c, 0, 0, left[c], core)
        forward(c, 4, 0, left[c], right[c], core)
        forward(c, 8, 0, left[c], rings[c], other)
        arrived(c, 3, 1, right[c], core)
        forward(c, 5, 1, right[c], left[c], core)
        forward(c, 11, 1, right[c], rings[c], other)
    for c in range(2):
        arrived(c, 1, 1, left[c], core)
        forward(c, 9, 1, left[c], rings[c], other)
        arrived(c, 2, 0, right[c], core)
        forward(c, 10, 0, right[c], rings[c], other)
    for c in range(2):
        arrived(c, 4, 0, far[c], core)
        forward(c, 12, 0, far[c], rings[c], other)
        arrived(c, 5, 1, far[c], core)
        forward(c, 13, 1, far[c], rings[c], other)
    for c in range(2):
        for i, h, src in (
            (6, 0, rings[c]),
            (7, 1, rings[c]),
            (8, 0, left[c]),
            (9, 1, left[c]),
            (10, 0, right[c]),
            (11, 1, right[c]),
            (12, 0, far[c]),
            (13, 1, far[c]),
        ):
            arrived(c, i, h, src, other)
        for n, (by, flip) in enumerate(others):
            ref = (iy, ix)[c].at[shift(rings[c], -by, 4), other if flip else core]
            remote(ref, ref, id_send.at[c, n], id_recv.at[c, n], member(c, rings[c], other)).wait_recv()
    for copy in started:
        copy.wait_send()
    for copy in kept:
        copy.wait()


def gather(p_tiles, q_tiles, ids):
    records = jax.ShapeDtypeStruct((4, 2, 4, RECORD, 128), BF16)
    numbers = jax.ShapeDtypeStruct((4, 2, 8, 128), jnp.int32)
    return pl.pallas_call(
        gather_kernel,
        name="gather",
        out_shape=(records, records, numbers, numbers),
        in_specs=[VMEM, VMEM, ANY],
        out_specs=(ANY,) * 4,
        scratch_shapes=[
            pltpu.VMEM((2, 4, RECORD, 128), BF16),
            pltpu.SemaphoreType.DMA((2, 14)),
            pltpu.SemaphoreType.DMA((2, 14)),
            pltpu.SemaphoreType.DMA((4,)),
            pltpu.SemaphoreType.DMA((2, 7)),
            pltpu.SemaphoreType.DMA((2, 7)),
        ],
        compiler_params=pltpu.CompilerParams(
            collective_id=0, has_side_effects=True, vmem_limit_bytes=32 << 20
        ),
    )(p_tiles, q_tiles, ids)


def fold_kernel(iy, ix, gy, gx, out, held, total, sem_in, sem_out):
    x, y, _, core = place()
    x_high, x_low = lax.div(x, 2), lax.rem(x, 2)
    loads = [
        [pltpu.make_async_copy(g.at[s // 2, s % 2], held.at[c, s], sem_in.at[c, s]) for s in range(8)]
        for c, g in enumerate((gy, gx))
    ]
    for c in range(2):
        for s in range(8):
            loads[c][s].start()

    @pl.loop(0, 129)
    def _(n):
        for c in range(2):
            total[c, n] = jnp.zeros((64, 128), F32)

    stores = []
    for c, (ids, g) in enumerate(((iy, gy), (ix, gx))):

        @pl.loop(0, 8)
        def _(s, c=c, ids=ids, g=g):
            ring, who = lax.div(s, 2), lax.rem(s, 2)
            pltpu.make_async_copy(g.at[ring, who], held.at[c, s], sem_in.at[c, s]).wait()

            @pl.loop(0, 4)
            def _(f):
                spots = []
                for l in range(6):
                    tile = ids[ring, who, f, 2 + l]
                    j = lax.rem(tile, 4)
                    tile_y, tile_x = lax.div(tile, 8), lax.rem(lax.div(tile, 4), 2)
                    mine, stop = (tile_y == y, tile_x) if c == 0 else (tile_x == x_low, tile_y)
                    spots.append((mine, j * 32 + stop * 8))
                for k in range(2):
                    tile = ids[ring, who, f, k]
                    tile_x = lax.div(tile, 16)
                    tile_z = lax.rem(lax.div(tile, 2), 8)
                    here = lax.rem(tile, 2) == core
                    if c == 1:
                        here = jnp.logical_and(here, tile_x == x_high)
                    base = tile_z + (tile_x * 16 if c == 0 else 0)

                    @pl.when(here)
                    def _(k=k, base=base):
                        product = jnp.dot(
                            held[c, s, f, 256:RECORD, :],
                            held[c, s, f, k * 128 : (k + 1) * 128, :],
                            preferred_element_type=F32,
                        )
                        for l, (mine, spot) in enumerate(spots):
                            n = jnp.where(mine, spot + base, 128)
                            total[c, n] += product[l * 64 : (l + 1) * 64]

        store = pltpu.make_async_copy(total.at[c, pl.ds(0, 128)], out.at[c], sem_out.at[c])
        store.start()
        stores.append(store)
    for store in stores:
        store.wait()


def fold(iy, ix, gy, gx):
    return pl.pallas_call(
        fold_kernel,
        name="fold",
        out_shape=jax.ShapeDtypeStruct((2, 128, 64, 128), F32),
        in_specs=[SMEM, SMEM, ANY, ANY],
        out_specs=ANY,
        scratch_shapes=[
            pltpu.VMEM((2, 8, 4, RECORD, 128), BF16),
            pltpu.VMEM((2, 129, 64, 128), F32),
            pltpu.SemaphoreType.DMA((2, 8)),
            pltpu.SemaphoreType.DMA((2,)),
        ],
        compiler_params=pltpu.CompilerParams(vmem_limit_bytes=48 << 20),
    )(iy, ix, gy, gx)


def reduce_kernel(part_hbm, out, part, near, full, zbuf, load, s_send, s_recv, z_send, z_recv):
    x, y, z, core = place()
    rings = (x, y)

    def member(c, pos):
        return device(pos, y, z, core) if c == 0 else device(x, pos, z, core)

    ends = [[member(c, shift(rings[c], d, 4)) for d in (1, -1)] for c in range(2)]
    z_ends = [device(x, y, shift(z, d, 8), core) for d in (1, -1)]
    loads = {}
    for j in range(4):
        for c in range(2):
            loads[c, j] = pltpu.make_async_copy(part_hbm.at[c, j], part.at[c, j], load.at[c, j])
            loads[c, j].start()
    greet(ends[0] + ends[1] + z_ends)

    started = []
    pending = {}

    def launch(key, copy):
        copy.start()
        started.append(copy)
        pending[key] = copy

    signs = (1, -1)

    def first(c, d, j):
        at = pl.ds(4 * d, 4)
        return remote(
            part.at[c, j, shift(rings[c], 2, 4), at],
            near.at[c, d, j],
            s_send.at[c, d, j, 0],
            s_recv.at[c, d, j, 0],
            ends[c][d],
        )

    def second(c, d, j, half):
        at = pl.ds(4 * half, 4)
        n = 2 if half == d else 1
        return remote(
            part.at[c, j, shift(rings[c], signs[d], 4), at],
            full.at[c, d, j, at],
            s_send.at[c, d, j, n],
            s_recv.at[c, d, j, n],
            ends[c][d],
        )

    def along_z(c, d, j, step):
        target = shift(z, signs[d] * (5 - step), 8)
        rows = pl.ds(32 * d, 32) if step == 1 else pl.ds(0, 64)
        return remote(
            part.at[c, j, rings[c], target, rows],
            zbuf.at[c, d, j, step - 1, rows],
            z_send.at[c, d, j, step - 1],
            z_recv.at[c, d, j, step - 1],
            z_ends[d],
        )

    both = [(c, d) for c in range(2) for d in range(2)]

    def open_chunk(j):
        for c in range(2):
            loads[c, j].wait()
        for c, d in both:
            launch(("first", c, d, j), first(c, d, j))
        for c, d in both:
            launch(("direct", c, d, j), second(c, d, j, 1 - d))

    def relay_chunk(j):
        for c, d in both:
            pending["first", c, d, j].wait_recv()
            spot = shift(rings[c], signs[d], 4)
            part[c, j, spot, 4 * d : 4 * d + 4] += near[c, d, j]
            launch(("relay", c, d, j), second(c, d, j, d))

    def close_chunk(j):
        for c, d in both:
            pending["direct", c, d, j].wait_recv()
            pending["relay", c, d, j].wait_recv()
        for c in range(2):
            part[c, j, rings[c]] += full[c, 0, j] + full[c, 1, j]

    def z_step(j, step):
        for c, d in both:
            if step > 1:
                pending["z", c, d, j, step - 1].wait_recv()
                target = shift(z, signs[d] * (5 - step), 8)
                rows = pl.ds(32 * d, 32) if step == 2 else pl.ds(0, 64)
                part[c, j, rings[c], target, rows] += zbuf[c, d, j, step - 2, rows]
            if step < 5:
                launch(("z", c, d, j, step), along_z(c, d, j, step))

    def finish_chunk(j):
        tiles = []
        for c in range(2):
            for d in range(2):
                pending["z", c, d, j, 4].wait_recv()
            tiles.append(part[c, j, rings[c], z] + zbuf[c, 0, j, 3] + zbuf[c, 1, j, 3])
        out[:, j * 128 : (j + 1) * 128] = jnp.concatenate(tiles, axis=0).T

    for tick in range(5):
        if tick < 4:
            open_chunk(tick)
        if tick > 0:
            z_step(tick - 1, 1)
            z_step(tick - 1, 2)
        if tick < 4:
            relay_chunk(tick)
        if tick > 0:
            z_step(tick - 1, 3)
            z_step(tick - 1, 4)
            finish_chunk(tick - 1)
        if tick < 4:
            close_chunk(tick)
    for copy in started:
        copy.wait_send()


def reduce(partial):
    return pl.pallas_call(
        reduce_kernel,
        name="reduce",
        out_shape=jax.ShapeDtypeStruct((128, 512), F32),
        in_specs=[ANY],
        out_specs=VMEM,
        scratch_shapes=[
            pltpu.VMEM((2, 4, 4, 8, 64, 128), F32),
            pltpu.VMEM((2, 2, 4, 4, 64, 128), F32),
            pltpu.VMEM((2, 2, 4, 8, 64, 128), F32),
            pltpu.VMEM((2, 2, 4, 4, 64, 128), F32),
            pltpu.SemaphoreType.DMA((2, 4)),
            pltpu.SemaphoreType.DMA((2, 2, 4, 3)),
            pltpu.SemaphoreType.DMA((2, 2, 4, 3)),
            pltpu.SemaphoreType.DMA((2, 2, 4, 4)),
            pltpu.SemaphoreType.DMA((2, 2, 4, 4)),
        ],
        compiler_params=pltpu.CompilerParams(
            collective_id=1, has_side_effects=True, vmem_limit_bytes=48 << 20
        ),
    )(partial.reshape(2, 4, 4, 8, 64, 128))


def body(p_tiles, p_cols, q_tiles, q_cols):
    ids = jnp.pad(jnp.concatenate([p_cols, q_cols], axis=1), ((0, 4), (0, 120)))
    gy, gx, iy, ix = gather(p_tiles, q_tiles, ids)
    return reduce(fold(iy, ix, gy, gx))


def solution(mesh):
    placed = (
        P(("row", "col"), None, None, None),
        P(("row", "col"), None),
        P(("row", "col"), None, None, None),
        P(("row", "col"), None),
    )
    return jax.shard_map(
        body, mesh=mesh, in_specs=placed, out_specs=P("row", "col"), check_vma=False
    )
```

```python
import jax
import jax.numpy as jnp
from jax import lax
from jax.experimental import pallas as pl
from jax.experimental.pallas import tpu as pltpu
from jax.sharding import PartitionSpec as P

MESH = pl.DeviceIdType.MESH
BF16, F32 = jnp.bfloat16, jnp.float32
ANY = pl.BlockSpec(memory_space=pl.ANY)
VMEM = pl.BlockSpec(memory_space=pltpu.VMEM)
RECORD = 640
LOAD = 48
NONE = 8 * LOAD


def place():
    row, col = lax.axis_index("row"), lax.axis_index("col")
    core, z = lax.rem(row, 2), lax.rem(lax.div(row, 2), 8)
    x = lax.div(row, 16) * 2 + lax.rem(col, 2)
    return x, lax.div(col, 2), z, core


def device(x, y, z, core):
    return (lax.div(x, 2) * 16 + z * 2 + core, y * 2 + lax.rem(x, 2))


def shift(v, by, n):
    return lax.rem(v + (by + n), n)


def remote(src, dst, send, recv, where):
    return pltpu.make_async_remote_copy(
        src_ref=src, dst_ref=dst, send_sem=send, recv_sem=recv, device_id=where, device_id_type=MESH
    )


def greet(partners):
    barrier = pltpu.get_barrier_semaphore()
    for partner in partners:
        pl.semaphore_signal(barrier, inc=1, device_id=partner, device_id_type=MESH)
    pl.semaphore_wait(barrier, len(partners))


def kernel(
    p_hbm, q_hbm, id_hbm, out,
    p_in, q_in, held, ids, table, marks, run, part, near, full, zbuf,
    in_sem, g_send, g_recv, id_send, id_recv, s_send, s_recv, z_send, z_recv,
):
    x, y, z, core = place()
    other = 1 - core
    gather_rings, reduce_rings = (y, x), (x, y)

    def along_y(pos, who):
        return device(x, pos, z, who)

    def along_x(pos, who):
        return device(pos, y, z, who)

    gather_member, reduce_member = (along_y, along_x), (along_x, along_y)
    z_ends = [device(x, y, shift(z, d, 8), core) for d in (1, -1)]
    others = [(by, flip) for by in range(4) for flip in range(2) if by or flip]

    inputs = []
    for f in range(4):
        inputs.append(pltpu.make_async_copy(q_hbm.at[f], q_in.at[f], in_sem.at[f]))
    inputs.append(pltpu.make_async_copy(p_hbm, p_in, in_sem.at[4]))
    inputs.append(pltpu.make_async_copy(id_hbm, ids.at[0, 0], in_sem.at[5]))
    inputs.append(pltpu.make_async_copy(id_hbm, ids.at[1, 0], in_sem.at[6]))
    for copy in inputs:
        copy.start()

    partners = [along_y(shift(y, by, 4), other if flip else core) for by, flip in others]
    partners += [along_x(shift(x, by, 4), other if flip else core) for by, flip in others if by]
    greet(partners + z_ends)

    started = []

    def launch(copy):
        copy.start()
        started.append(copy)
        return copy

    slot = {0: 0, 1: 2, 3: 4, 2: 6}
    inputs[5].wait()
    inputs[6].wait()
    for c in range(2):
        for n, (by, flip) in enumerate(others):
            who = gather_member[c](shift(gather_rings[c], by, 4), other if flip else core)
            launch(remote(ids.at[c, 0], ids.at[c, slot[by] + flip], id_send.at[c, n], id_recv.at[c, n], who))

    def stage_block(f):
        inputs[f].wait()
        for c in range(2):
            for k in range(2):
                held[c, 0, f, k * 128 : (k + 1) * 128, :] = p_in[f, k]
        for l in range(6):
            flipped = q_in[f, l].T
            for c in range(2):
                held[c, 0, f, 256 + l * 64 : 320 + l * 64, :] = flipped[c * 64 : c * 64 + 64]

    def send(c, i, h, source, target, by, flip=False):
        at = pl.ds(h * 2, 2)
        who = gather_member[c](shift(gather_rings[c], by, 4), other if flip else core)
        launch(remote(held.at[c, source, at], held.at[c, target, at], g_send.at[c, i], g_recv.at[c, i], who))

    def arrived(c, i, h, target):
        ref = held.at[c, target, pl.ds(h * 2, 2)]
        remote(ref, ref, g_send.at[c, i], g_recv.at[c, i], gather_member[c](gather_rings[c], other)).wait_recv()

    inputs[4].wait()
    for f in range(2):
        stage_block(f)
    for c in range(2):
        send(c, 0, 0, 0, 2, 1)
        send(c, 6, 0, 0, 1, 0, True)
    for f in range(2, 4):
        stage_block(f)
    for c in range(2):
        send(c, 3, 1, 0, 4, -1)
        send(c, 1, 1, 0, 2, 1)
        send(c, 2, 0, 0, 4, -1)
        send(c, 7, 1, 0, 1, 0, True)

    for c in range(2):
        for n, (by, flip) in enumerate(others):
            ref = ids.at[c, slot[by] + flip]
            remote(ref, ref, id_send.at[c, n], id_recv.at[c, n], gather_member[c](gather_rings[c], other)).wait_recv()
    lane = lax.broadcasted_iota(jnp.int32, (8, 128), 1)
    below = lax.broadcasted_iota(jnp.int32, (LOAD, 128), 0)
    beside = lax.broadcasted_iota(jnp.int32, (LOAD, 128), 1)
    for c in range(2):
        rows = jnp.concatenate([ids[c, t, 0:1, :] for t in range(8)], axis=0)
        cols = jnp.concatenate([ids[c, t, 1:2, :] for t in range(8)], axis=0)
        mine = jnp.logical_and((rows & 1) == core, lane < LOAD)
        tile_x, tile_z = rows >> 4, (rows >> 1) & 7
        stop_y, stop_x, j = cols >> 3, (cols >> 2) & 1, cols & 3
        if c == 0:
            mine = jnp.logical_and(mine, stop_y == y)
            target = j * 32 + (tile_x * 2 + stop_x) * 8 + tile_z
        else:
            mine = jnp.logical_and(mine, jnp.logical_and(tile_x == lax.div(x, 2), stop_x == lax.rem(x, 2)))
            target = j * 32 + stop_y * 8 + tile_z
        target = jnp.where(mine, target, -1)
        flat = jnp.where(mine, target, -2).T[0:LOAD]
        last = jnp.full((1, 128), -1, jnp.int32)
        for t in range(8):
            same = jnp.broadcast_to(flat[:, t : t + 1], (LOAD, 128)) == beside
            last = jnp.maximum(last, jnp.max(jnp.where(same, below + t * LOAD, -1), axis=0, keepdims=True))
            found = jnp.full((1, 128), -1, jnp.int32)
            mark = jnp.broadcast_to(target[t : t + 1], (LOAD, 128))
            for u in range(t + 1):
                same = jnp.broadcast_to(flat[:, u : u + 1], (LOAD, 128)) == mark
                if u == t:
                    same = jnp.logical_and(same, below < beside)
                found = jnp.maximum(found, jnp.max(jnp.where(same, below + u * LOAD, -1), axis=0, keepdims=True))
            table[c, t : t + 1, :] = jnp.where(found < 0, NONE, found)
        table[c, 8:9, :] = jnp.where(last < 0, NONE, last)
        table[c, 9:16, :] = jnp.zeros((7, 128), jnp.int32)
        run[c, NONE] = jnp.zeros((64, 128), F32)
    copy = pltpu.make_async_copy(table, marks, in_sem.at[7])
    copy.start()
    copy.wait()

    def multiply(c, t):
        @pl.loop(0, 4)
        def _(f):
            pair = jnp.concatenate([held[c, t, f, 0:128, :], held[c, t, f, 128:256, :]], axis=1)
            product = jnp.dot(held[c, t, f, 256:RECORD, :], pair, preferred_element_type=F32)
            for k in range(2):
                sums = []
                for l in range(6):
                    before = run[c, marks[c, t, f * 12 + k * 6 + l]]
                    sums.append(product[l * 64 : (l + 1) * 64, k * 128 : (k + 1) * 128] + before)
                for l in range(6):
                    run[c, t * LOAD + f * 12 + k * 6 + l] = sums[l]

    for c in range(2):
        multiply(c, 0)
    for c in range(2):
        arrived(c, 6, 0, 1)
        arrived(c, 7, 1, 1)
        multiply(c, 1)
    for c in range(2):
        arrived(c, 0, 0, 2)
        send(c, 4, 0, 2, 6, 1)
        send(c, 8, 0, 2, 3, 0, True)
        arrived(c, 3, 1, 4)
        send(c, 5, 1, 4, 6, -1)
        send(c, 11, 1, 4, 5, 0, True)
    for c in range(2):
        arrived(c, 1, 1, 2)
        send(c, 9, 1, 2, 3, 0, True)
        arrived(c, 2, 0, 4)
        send(c, 10, 0, 4, 5, 0, True)
    for c in range(2):
        multiply(c, 2)
    for c in range(2):
        arrived(c, 8, 0, 3)
        arrived(c, 9, 1, 3)
        multiply(c, 3)
    for c in range(2):
        multiply(c, 4)
    for c in range(2):
        arrived(c, 10, 0, 5)
        arrived(c, 11, 1, 5)
        multiply(c, 5)
    for c in range(2):
        arrived(c, 4, 0, 6)
        send(c, 12, 0, 6, 7, 0, True)
        arrived(c, 5, 1, 6)
        send(c, 13, 1, 6, 7, 0, True)
    for c in range(2):
        multiply(c, 6)
    for c in range(2):
        arrived(c, 12, 0, 7)
        arrived(c, 13, 1, 7)
        multiply(c, 7)

    rings, signs = reduce_rings, (1, -1)
    ends = [[reduce_member[c](shift(rings[c], d, 4), core) for d in signs] for c in range(2)]
    pending = {}

    def first(c, d, j):
        at = pl.ds(4 * d, 4)
        return remote(
            part.at[c, j, shift(rings[c], 2, 4), at],
            near.at[c, d, j],
            s_send.at[c, d, j, 0],
            s_recv.at[c, d, j, 0],
            ends[c][d],
        )

    def second(c, d, j, half):
        at = pl.ds(4 * half, 4)
        n = 2 if half == d else 1
        return remote(
            part.at[c, j, shift(rings[c], signs[d], 4), at],
            full.at[c, d, j, at],
            s_send.at[c, d, j, n],
            s_recv.at[c, d, j, n],
            ends[c][d],
        )

    def along_z(c, d, j, step):
        target = shift(z, signs[d] * (5 - step), 8)
        rows = pl.ds(32 * d, 32) if step == 1 else pl.ds(0, 64)
        return remote(
            part.at[c, j, rings[c], target, rows],
            zbuf.at[c, d, j, step - 1, rows],
            z_send.at[c, d, j, step - 1],
            z_recv.at[c, d, j, step - 1],
            z_ends[d],
        )

    both = [(c, d) for c in range(2) for d in range(2)]

    def open_chunk(j):
        for c in range(2):

            @pl.loop(0, 32)
            def _(n, c=c):
                part[c, j, lax.div(n, 8), lax.rem(n, 8)] = run[c, marks[c, 8, j * 32 + n]]

        for c, d in both:
            pending["first", c, d, j] = launch(first(c, d, j))
        for c, d in both:
            pending["direct", c, d, j] = launch(second(c, d, j, 1 - d))

    def relay_chunk(j):
        for c, d in both:
            pending["first", c, d, j].wait_recv()
            spot = shift(rings[c], signs[d], 4)
            part[c, j, spot, 4 * d : 4 * d + 4] += near[c, d, j]
            pending["relay", c, d, j] = launch(second(c, d, j, d))

    def close_chunk(j):
        for c, d in both:
            pending["direct", c, d, j].wait_recv()
            pending["relay", c, d, j].wait_recv()
        for c in range(2):
            part[c, j, rings[c]] += full[c, 0, j] + full[c, 1, j]

    def z_step(j, step):
        for c, d in both:
            if step > 1:
                pending["z", c, d, j, step - 1].wait_recv()
                target = shift(z, signs[d] * (5 - step), 8)
                rows = pl.ds(32 * d, 32) if step == 2 else pl.ds(0, 64)
                part[c, j, rings[c], target, rows] += zbuf[c, d, j, step - 2, rows]
            if step < 5:
                pending["z", c, d, j, step] = launch(along_z(c, d, j, step))

    def finish_chunk(j):
        tiles = []
        for c in range(2):
            for d in range(2):
                pending["z", c, d, j, 4].wait_recv()
            tiles.append(part[c, j, rings[c], z] + zbuf[c, 0, j, 3] + zbuf[c, 1, j, 3])
        out[:, j * 128 : (j + 1) * 128] = jnp.concatenate(tiles, axis=0).T

    for tick in range(5):
        if tick < 4:
            open_chunk(tick)
        if tick > 0:
            z_step(tick - 1, 1)
            z_step(tick - 1, 2)
        if tick < 4:
            relay_chunk(tick)
        if tick > 0:
            z_step(tick - 1, 3)
            z_step(tick - 1, 4)
            finish_chunk(tick - 1)
        if tick < 4:
            close_chunk(tick)
    for copy in started:
        copy.wait_send()


def body(p_tiles, p_cols, q_tiles, q_cols):
    rows = jnp.broadcast_to(p_cols[:, :, None], (4, 2, 6)).reshape(1, LOAD)
    cols = jnp.broadcast_to(q_cols[:, None, :], (4, 2, 6)).reshape(1, LOAD)
    ids = jnp.pad(jnp.concatenate([rows, cols], axis=0), ((0, 6), (0, 128 - LOAD)))
    dma = pltpu.SemaphoreType.DMA
    return pl.pallas_call(
        kernel,
        name="coarse",
        out_shape=jax.ShapeDtypeStruct((128, 512), F32),
        in_specs=[ANY, ANY, ANY],
        out_specs=VMEM,
        scratch_shapes=[
            pltpu.VMEM((4, 2, 128, 128), BF16),
            pltpu.VMEM((4, 6, 128, 128), BF16),
            pltpu.VMEM((2, 8, 4, RECORD, 128), BF16),
            pltpu.VMEM((2, 8, 8, 128), jnp.int32),
            pltpu.VMEM((2, 16, 128), jnp.int32),
            pltpu.SMEM((2, 16, 128), jnp.int32),
            pltpu.VMEM((2, NONE + 1, 64, 128), F32),
            pltpu.VMEM((2, 4, 4, 8, 64, 128), F32),
            pltpu.VMEM((2, 2, 4, 4, 64, 128), F32),
            pltpu.VMEM((2, 2, 4, 8, 64, 128), F32),
            pltpu.VMEM((2, 2, 4, 4, 64, 128), F32),
            dma((8,)),
            dma((2, 14)),
            dma((2, 14)),
            dma((2, 7)),
            dma((2, 7)),
            dma((2, 2, 4, 3)),
            dma((2, 2, 4, 3)),
            dma((2, 2, 4, 4)),
            dma((2, 2, 4, 4)),
        ],
        compiler_params=pltpu.CompilerParams(
            collective_id=0, has_side_effects=True, vmem_limit_bytes=60 << 20
        ),
    )(p_tiles, q_tiles, ids)


def solution(mesh):
    placed = (
        P(("row", "col"), None, None, None),
        P(("row", "col"), None),
        P(("row", "col"), None, None, None),
        P(("row", "col"), None),
    )
    return jax.shard_map(
        body, mesh=mesh, in_specs=placed, out_specs=P("row", "col"), check_vma=False
    )
```

```python
import jax
import jax.numpy as jnp
from jax import lax
from jax.experimental import pallas as pl
from jax.experimental.pallas import tpu as pltpu
from jax.sharding import PartitionSpec as P

MESH = pl.DeviceIdType.MESH
BF16, F32 = jnp.bfloat16, jnp.float32
ANY = pl.BlockSpec(memory_space=pl.ANY)
VMEM = pl.BlockSpec(memory_space=pltpu.VMEM)
RECORD = 640
LOAD = 48
NONE = 8 * LOAD
CHUNKS = (
    (0, 0, 64, True),
    (1, 0, 64, True),
    (2, 0, 64, True),
)
WIDE = ((3, 0, 64),)
ORDER = (
    ("load", 0), ("first", 0), ("wload", 0), ("wz", 0, 1), ("load", 1), ("direct", 0), ("load", 2), ("first", 2),
    ("wz", 0, 2), ("relay", 0), ("first", 1), ("wz", 0, 3), ("relay", 2), ("close", 0), ("z", 0, 1), ("direct", 2),
    ("direct", 1), ("wz", 0, 4), ("relay", 1), ("close", 2), ("z", 2, 1), ("z", 0, 2), ("z", 2, 2), ("wring", 0),
    ("z", 0, 3), ("close", 1), ("z", 1, 1), ("z", 2, 3), ("z", 1, 2), ("z", 2, 4), ("wrelay", 0), ("z", 1, 3),
    ("z", 0, 4), ("z", 1, 4), ("finish", 0), ("wfinish", 0), ("finish", 2), ("finish", 1),
)


def place():
    row, col = lax.axis_index("row"), lax.axis_index("col")
    core, z = lax.rem(row, 2), lax.rem(lax.div(row, 2), 8)
    x = lax.div(row, 16) * 2 + lax.rem(col, 2)
    return x, lax.div(col, 2), z, core


def device(x, y, z, core):
    return (lax.div(x, 2) * 16 + z * 2 + core, y * 2 + lax.rem(x, 2))


def shift(v, by, n):
    return lax.rem(v + (by + n), n)


def remote(src, dst, send, recv, where):
    return pltpu.make_async_remote_copy(
        src_ref=src, dst_ref=dst, send_sem=send, recv_sem=recv, device_id=where, device_id_type=MESH
    )


def greet(partners):
    barrier = pltpu.get_barrier_semaphore()
    for partner in partners:
        pl.semaphore_signal(barrier, inc=1, device_id=partner, device_id_type=MESH)
    pl.semaphore_wait(barrier, len(partners))


def kernel(
    p_hbm, q_hbm, id_hbm, out,
    p_in, q_in, held, ids, table, marks, run, part, near, full, zbuf, zall, done, wbuf, ring,
    in_sem, g_send, g_recv, id_send, id_recv, s_send, s_recv, z_send, z_recv, d_send, d_recv, w_send, w_recv, r_send, r_recv,
):
    x, y, z, core = place()
    other = 1 - core
    gather_rings, reduce_rings = (y, x), (x, y)

    def along_y(pos, who):
        return device(x, pos, z, who)

    def along_x(pos, who):
        return device(pos, y, z, who)

    gather_member, reduce_member = (along_y, along_x), (along_x, along_y)
    z_ends = [device(x, y, shift(z, d, 8), core) for d in (1, -1)]
    z_ring = [device(x, y, shift(z, d, 8), core) for d in range(1, 8)]
    others = [(by, flip) for by in range(4) for flip in range(2) if by or flip]

    inputs = []
    for f in range(4):
        inputs.append(pltpu.make_async_copy(q_hbm.at[f], q_in.at[f], in_sem.at[f]))
    inputs.append(pltpu.make_async_copy(p_hbm, p_in, in_sem.at[4]))
    inputs.append(pltpu.make_async_copy(id_hbm, ids.at[0, 0], in_sem.at[5]))
    inputs.append(pltpu.make_async_copy(id_hbm, ids.at[1, 0], in_sem.at[6]))
    for copy in inputs:
        copy.start()

    partners = [along_y(shift(y, by, 4), other if flip else core) for by, flip in others]
    partners += [along_x(shift(x, by, 4), other if flip else core) for by, flip in others if by]
    greet(partners + z_ring)

    started = []

    def launch(copy):
        copy.start()
        started.append(copy)
        return copy

    slot = {0: 0, 1: 2, 3: 4, 2: 6}
    inputs[5].wait()
    inputs[6].wait()
    for c in range(2):
        for n, (by, flip) in enumerate(others):
            who = gather_member[c](shift(gather_rings[c], by, 4), other if flip else core)
            launch(remote(ids.at[c, 0], ids.at[c, slot[by] + flip], id_send.at[c, n], id_recv.at[c, n], who))

    def stage_block(f):
        inputs[f].wait()
        for c in range(2):
            for k in range(2):
                held[c, 0, f, k * 128 : (k + 1) * 128, :] = p_in[f, k]
        for l in range(6):
            flipped = q_in[f, l].T
            for c in range(2):
                held[c, 0, f, 256 + l * 64 : 320 + l * 64, :] = flipped[c * 64 : c * 64 + 64]

    def send(c, i, h, source, target, by, flip=False):
        at = pl.ds(h * 2, 2)
        who = gather_member[c](shift(gather_rings[c], by, 4), other if flip else core)
        launch(remote(held.at[c, source, at], held.at[c, target, at], g_send.at[c, i], g_recv.at[c, i], who))

    def arrived(c, i, h, target):
        ref = held.at[c, target, pl.ds(h * 2, 2)]
        remote(ref, ref, g_send.at[c, i], g_recv.at[c, i], gather_member[c](gather_rings[c], other)).wait_recv()

    inputs[4].wait()
    for f in range(2):
        stage_block(f)
    for c in range(2):
        send(c, 0, 0, 0, 2, 1)
        send(c, 6, 0, 0, 1, 0, True)
    for f in range(2, 4):
        stage_block(f)
    for c in range(2):
        send(c, 3, 1, 0, 4, -1)
        send(c, 1, 1, 0, 2, 1)
        send(c, 2, 0, 0, 4, -1)
        send(c, 7, 1, 0, 1, 0, True)

    for c in range(2):
        for n, (by, flip) in enumerate(others):
            ref = ids.at[c, slot[by] + flip]
            remote(ref, ref, id_send.at[c, n], id_recv.at[c, n], gather_member[c](gather_rings[c], other)).wait_recv()
    lane = lax.broadcasted_iota(jnp.int32, (8, 128), 1)
    below = lax.broadcasted_iota(jnp.int32, (LOAD, 128), 0)
    beside = lax.broadcasted_iota(jnp.int32, (LOAD, 128), 1)
    for c in range(2):
        rows = jnp.concatenate([ids[c, t, 0:1, :] for t in range(8)], axis=0)
        cols = jnp.concatenate([ids[c, t, 1:2, :] for t in range(8)], axis=0)
        mine = jnp.logical_and((rows & 1) == core, lane < LOAD)
        tile_x, tile_z = rows >> 4, (rows >> 1) & 7
        stop_y, stop_x, j = cols >> 3, (cols >> 2) & 1, cols & 3
        if c == 0:
            mine = jnp.logical_and(mine, stop_y == y)
            target = j * 32 + (tile_x * 2 + stop_x) * 8 + tile_z
        else:
            mine = jnp.logical_and(mine, jnp.logical_and(tile_x == lax.div(x, 2), stop_x == lax.rem(x, 2)))
            target = j * 32 + stop_y * 8 + tile_z
        target = jnp.where(mine, target, -1)
        flat = jnp.where(mine, target, -2).T[0:LOAD]
        last = jnp.full((1, 128), -1, jnp.int32)
        for t in range(8):
            same = jnp.broadcast_to(flat[:, t : t + 1], (LOAD, 128)) == beside
            last = jnp.maximum(last, jnp.max(jnp.where(same, below + t * LOAD, -1), axis=0, keepdims=True))
            found = jnp.full((1, 128), -1, jnp.int32)
            mark = jnp.broadcast_to(target[t : t + 1], (LOAD, 128))
            for u in range(t + 1):
                same = jnp.broadcast_to(flat[:, u : u + 1], (LOAD, 128)) == mark
                if u == t:
                    same = jnp.logical_and(same, below < beside)
                found = jnp.maximum(found, jnp.max(jnp.where(same, below + u * LOAD, -1), axis=0, keepdims=True))
            table[c, t : t + 1, :] = jnp.where(found < 0, NONE, found)
        table[c, 8:9, :] = jnp.where(last < 0, NONE, last)
        table[c, 9:16, :] = jnp.zeros((7, 128), jnp.int32)
        run[c, NONE] = jnp.zeros((64, 128), F32)
    copy = pltpu.make_async_copy(table, marks, in_sem.at[7])
    copy.start()
    copy.wait()

    def multiply(c, t):
        @pl.loop(0, 4)
        def _(f):
            pair = jnp.concatenate([held[c, t, f, 0:128, :], held[c, t, f, 128:256, :]], axis=1)
            product = jnp.dot(held[c, t, f, 256:RECORD, :], pair, preferred_element_type=F32)
            for k in range(2):
                sums = []
                for l in range(6):
                    before = run[c, marks[c, t, f * 12 + k * 6 + l]]
                    sums.append(product[l * 64 : (l + 1) * 64, k * 128 : (k + 1) * 128] + before)
                for l in range(6):
                    run[c, t * LOAD + f * 12 + k * 6 + l] = sums[l]

    for c in range(2):
        multiply(c, 0)
    for c in range(2):
        arrived(c, 6, 0, 1)
        arrived(c, 7, 1, 1)
        multiply(c, 1)
    for c in range(2):
        arrived(c, 0, 0, 2)
        send(c, 4, 0, 2, 6, 1)
        send(c, 8, 0, 2, 3, 0, True)
        arrived(c, 3, 1, 4)
        send(c, 5, 1, 4, 6, -1)
        send(c, 11, 1, 4, 5, 0, True)
    for c in range(2):
        arrived(c, 1, 1, 2)
        send(c, 9, 1, 2, 3, 0, True)
        arrived(c, 2, 0, 4)
        send(c, 10, 0, 4, 5, 0, True)
    for c in range(2):
        multiply(c, 2)
    for c in range(2):
        arrived(c, 8, 0, 3)
        arrived(c, 9, 1, 3)
        multiply(c, 3)
    for c in range(2):
        multiply(c, 4)
    for c in range(2):
        arrived(c, 10, 0, 5)
        arrived(c, 11, 1, 5)
        multiply(c, 5)
    for c in range(2):
        arrived(c, 4, 0, 6)
        send(c, 12, 0, 6, 7, 0, True)
        arrived(c, 5, 1, 6)
        send(c, 13, 1, 6, 7, 0, True)
    for c in range(2):
        multiply(c, 6)
    for c in range(2):
        arrived(c, 12, 0, 7)
        arrived(c, 13, 1, 7)
        multiply(c, 7)

    rings, signs = reduce_rings, (1, -1)
    ends = [[reduce_member[c](shift(rings[c], d, 4), core) for d in signs] for c in range(2)]
    pending = {}

    def rows_of(i):
        _, start, count, _ = CHUNKS[i]
        return pl.ds(start, count)

    def first(c, d, i):
        j, at = CHUNKS[i][0], pl.ds(4 * d, 4)
        return remote(
            part.at[c, j, shift(rings[c], 2, 4), at, rows_of(i)],
            near.at[c, d, j, :, rows_of(i)],
            s_send.at[c, d, i, 0],
            s_recv.at[c, d, i, 0],
            ends[c][d],
        )

    def second(c, d, i, half):
        j, at = CHUNKS[i][0], pl.ds(4 * half, 4)
        n = 2 if half == d else 1
        return remote(
            part.at[c, j, shift(rings[c], signs[d], 4), at, rows_of(i)],
            full.at[c, d, j, at, rows_of(i)],
            s_send.at[c, d, i, n],
            s_recv.at[c, d, i, n],
            ends[c][d],
        )

    def along_z(c, d, i, step):
        j = CHUNKS[i][0]
        target = shift(z, signs[d] * (5 - step), 8)
        _, start, count, _ = CHUNKS[i]
        rows = pl.ds(start + d * count // 2, count // 2) if step == 1 else pl.ds(start, count)
        return remote(
            part.at[c, j, rings[c], target, rows],
            zbuf.at[c, d, j, step - 1, rows],
            z_send.at[c, d, i, step - 1],
            z_recv.at[c, d, i, step - 1],
            z_ends[d],
        )

    def straight(c, i, by):
        j = CHUNKS[i][0]
        target = shift(z, by, 8)
        return remote(
            part.at[c, j, rings[c], target, rows_of(i)],
            zall.at[c, by - 1, rows_of(i)],
            d_send.at[c, i, by - 1],
            d_recv.at[c, i, by - 1],
            device(x, y, target, core),
        )

    both = [(c, d) for c in range(2) for d in range(2)]

    def load(j, start, count):
        for c in range(2):

            @pl.loop(0, 32)
            def _(n, c=c):
                part[c, j, lax.div(n, 8), lax.rem(n, 8), start : start + count] = run[
                    c, marks[c, 8, j * 32 + n], start : start + count
                ]

    def send_first(i):
        for c, d in both:
            pending["first", c, d, i] = launch(first(c, d, i))

    def send_direct(i):
        for c, d in both:
            pending["direct", c, d, i] = launch(second(c, d, i, 1 - d))

    def relay_chunk(i):
        j, start, count, _ = CHUNKS[i]
        for c, d in both:
            pending["first", c, d, i].wait_recv()
            spot = shift(rings[c], signs[d], 4)
            part[c, j, spot, 4 * d : 4 * d + 4, start : start + count] += near[c, d, j, :, start : start + count]
            pending["relay", c, d, i] = launch(second(c, d, i, d))

    def close_chunk(i):
        j, start, count, _ = CHUNKS[i]
        for c, d in both:
            pending["direct", c, d, i].wait_recv()
            pending["relay", c, d, i].wait_recv()
        span = slice(start, start + count)
        for c in range(2):
            part[c, j, rings[c], :, span] += full[c, 0, j, :, span] + full[c, 1, j, :, span]

    def send_straight(i):
        for by in (4, 3, 5, 2, 6, 1, 7):
            for c in range(2):
                pending["straight", c, i, by] = launch(straight(c, i, by))

    def z_step(i, step):
        j, start, count, _ = CHUNKS[i]
        for c, d in both:
            if step > 1:
                pending["z", c, d, i, step - 1].wait_recv()
                target = shift(z, signs[d] * (5 - step), 8)
                rows = slice(start, start + count)
                if step == 2:
                    rows = slice(start + d * count // 2, start + (d + 1) * count // 2)
                part[c, j, rings[c], target, rows] += zbuf[c, d, j, step - 2, rows]
            pending["z", c, d, i, step] = launch(along_z(c, d, i, step))

    rows_done = [0] * 4

    def complete(j, count):
        rows_done[j] += count
        if rows_done[j] == 64:
            out[:, j * 128 : (j + 1) * 128] = done[j].T

    def finish(i):
        j, start, count, chained = CHUNKS[i]
        span = slice(start, start + count)
        for c in range(2):
            if chained:
                for d in range(2):
                    pending["z", c, d, i, 4].wait_recv()
                tile = part[c, j, rings[c], z, span] + zbuf[c, 0, j, 3, span] + zbuf[c, 1, j, 3, span]
            else:
                tile = part[c, j, rings[c], z, span]
                for by in range(1, 8):
                    pending["straight", c, i, by].wait_recv()
                    tile += zall[c, by - 1, span]
            done[j, c * 64 + start : c * 64 + start + count, :] = tile
        complete(j, count)

    def wide_z(s, step):
        j, start, count = WIDE[s]
        for c, d in both:
            target = shift(z, signs[d] * (5 - step), 8)
            low, size = (start + d * count // 2, count // 2) if step < 3 else (start, count)
            if step > 1:
                pending["wide", c, d, s, step - 1].wait_recv()
                part[c, j, :, target, low : low + size] += wbuf[c, d, step - 2, :, low : low + size]
            rows = pl.ds(low, size) if step == 1 else pl.ds(start, count)
            pending["wide", c, d, s, step] = launch(
                remote(
                    part.at[c, j, :, target, rows],
                    wbuf.at[c, d, step - 1, :, rows],
                    w_send.at[c, d, s, step - 1],
                    w_recv.at[c, d, s, step - 1],
                    z_ends[d],
                )
            )

    def wide_ring(s):
        j, start, count = WIDE[s]
        span = slice(start, start + count)
        for c in range(2):
            for d in range(2):
                pending["wide", c, d, s, 4].wait_recv()
            part[c, j, :, z, span] += wbuf[c, 0, 3, :, span] + wbuf[c, 1, 3, :, span]
            for d in range(2):
                half = pl.ds(start + d * count // 2, count // 2)
                pending["half", c, d, s] = launch(
                    remote(
                        part.at[c, j, shift(rings[c], 2, 4), z, half],
                        ring.at[0, c, d, half],
                        r_send.at[c, d, s, 0],
                        r_recv.at[c, d, s, 0],
                        ends[c][d],
                    )
                )

    def wide_relay(s):
        j, start, count = WIDE[s]
        rows = pl.ds(start, count)
        for c, d in both:
            pending["half", c, d, s].wait_recv()
            low, spot = start + d * count // 2, shift(rings[c], signs[d], 4)
            half = slice(low, low + count // 2)
            part[c, j, spot, z, half] += ring[0, c, d, half]
            pending["whole", c, d, s] = launch(
                remote(
                    part.at[c, j, spot, z, rows],
                    ring.at[1, c, d, rows],
                    r_send.at[c, d, s, 1],
                    r_recv.at[c, d, s, 1],
                    ends[c][d],
                )
            )

    def wide_finish(s):
        j, start, count = WIDE[s]
        span = slice(start, start + count)
        for c in range(2):
            for d in range(2):
                pending["whole", c, d, s].wait_recv()
            done[j, c * 64 + start : c * 64 + start + count, :] = (
                part[c, j, rings[c], z, span] + ring[1, c, 0, span] + ring[1, c, 1, span]
            )
        complete(j, count)

    steps = {
        "load": lambda i: load(*CHUNKS[i][:3]), "first": send_first, "direct": send_direct, "relay": relay_chunk,
        "close": close_chunk, "z": z_step, "straight": send_straight, "finish": finish,
        "wload": lambda i: load(*WIDE[i]), "wz": wide_z, "wring": wide_ring, "wrelay": wide_relay, "wfinish": wide_finish,
    }
    for step in ORDER:
        steps[step[0]](*step[1:])
    for copy in started:
        copy.wait_send()


def body(p_tiles, p_cols, q_tiles, q_cols):
    rows = jnp.broadcast_to(p_cols[:, :, None], (4, 2, 6)).reshape(1, LOAD)
    cols = jnp.broadcast_to(q_cols[:, None, :], (4, 2, 6)).reshape(1, LOAD)
    ids = jnp.pad(jnp.concatenate([rows, cols], axis=0), ((0, 6), (0, 128 - LOAD)))
    dma = pltpu.SemaphoreType.DMA
    return pl.pallas_call(
        kernel,
        name="coarse",
        out_shape=jax.ShapeDtypeStruct((128, 512), F32),
        in_specs=[ANY, ANY, ANY],
        out_specs=VMEM,
        scratch_shapes=[
            pltpu.VMEM((4, 2, 128, 128), BF16),
            pltpu.VMEM((4, 6, 128, 128), BF16),
            pltpu.VMEM((2, 8, 4, RECORD, 128), BF16),
            pltpu.VMEM((2, 8, 8, 128), jnp.int32),
            pltpu.VMEM((2, 16, 128), jnp.int32),
            pltpu.SMEM((2, 16, 128), jnp.int32),
            pltpu.VMEM((2, NONE + 1, 64, 128), F32),
            pltpu.VMEM((2, 4, 4, 8, 64, 128), F32),
            pltpu.VMEM((2, 2, 4, 4, 64, 128), F32),
            pltpu.VMEM((2, 2, 4, 8, 64, 128), F32),
            pltpu.VMEM((2, 2, 4, 4, 64, 128), F32),
            pltpu.VMEM((2, 7, 64, 128), F32),
            pltpu.VMEM((4, 128, 128), F32),
            pltpu.VMEM((2, 2, 4, 4, 64, 128), F32),
            pltpu.VMEM((2, 2, 2, 64, 128), F32),
            dma((8,)),
            dma((2, 14)),
            dma((2, 14)),
            dma((2, 7)),
            dma((2, 7)),
            dma((2, 2, len(CHUNKS), 3)),
            dma((2, 2, len(CHUNKS), 3)),
            dma((2, 2, len(CHUNKS), 4)),
            dma((2, 2, len(CHUNKS), 4)),
            dma((2, len(CHUNKS), 7)),
            dma((2, len(CHUNKS), 7)),
            dma((2, 2, len(WIDE), 4)),
            dma((2, 2, len(WIDE), 4)),
            dma((2, 2, len(WIDE), 2)),
            dma((2, 2, len(WIDE), 2)),
        ],
        compiler_params=pltpu.CompilerParams(
            collective_id=0, has_side_effects=True, vmem_limit_bytes=60 << 20
        ),
    )(p_tiles, q_tiles, ids)


def solution(mesh):
    placed = (
        P(("row", "col"), None, None, None),
        P(("row", "col"), None),
        P(("row", "col"), None, None, None),
        P(("row", "col"), None),
    )
    return jax.shard_map(
        body, mesh=mesh, in_specs=placed, out_specs=P("row", "col"), check_vma=False
    )
```

```python
import jax
import jax.numpy as jnp
from jax import lax
from jax.experimental import pallas as pl
from jax.experimental.pallas import tpu as pltpu
from jax.sharding import PartitionSpec as P

MESH = pl.DeviceIdType.MESH
BF16, F32 = jnp.bfloat16, jnp.float32
ANY = pl.BlockSpec(memory_space=pl.ANY)
VMEM = pl.BlockSpec(memory_space=pltpu.VMEM)
SMEM = pl.BlockSpec(memory_space=pltpu.SMEM)
RECORD = 640
LOAD = 48
NONE = 8 * LOAD
HALF = 32
BLOCKS = ((0, 256 + 6 * HALF), (256 + 6 * HALF, 6 * HALF))
CHUNKS = ((16, 16), (32, 16), (48, 16))
WIDE = ((0, 16),)
ORDER = (
    ("wload", 0), ("wz", 0, 1), ("mul", 0), ("load", 0), ("near", 0), ("first", 0), ("mul", 1), ("mul", 2),
    ("direct", 0), ("wz", 0, 2), ("mul", 3), ("mul", 4), ("far", 0), ("mul", 5), ("relay", 0), ("mul", 6),
    ("mul", 7), ("load", 1), ("first", 1), ("load", 2), ("direct", 1), ("wz", 0, 3), ("relay", 1), ("close", 0),
    ("first", 2), ("z", 0, 1), ("wz", 0, 4), ("direct", 2), ("z", 0, 2), ("close", 1), ("relay", 2), ("z", 1, 1),
    ("z", 0, 3), ("z", 1, 2), ("wring", 0), ("close", 2), ("z", 2, 1), ("z", 1, 3), ("z", 2, 2), ("z", 1, 4),
    ("z", 2, 3), ("z", 0, 4), ("wrelay", 0), ("finish", 1), ("z", 2, 4), ("finish", 0), ("wfinish", 0),
    ("finish", 2),
)


def place():
    row, col = lax.axis_index("row"), lax.axis_index("col")
    core, z = lax.rem(row, 2), lax.rem(lax.div(row, 2), 8)
    x = lax.div(row, 16) * 2 + lax.rem(col, 2)
    return x, lax.div(col, 2), z, core


def device(x, y, z, core):
    return (lax.div(x, 2) * 16 + z * 2 + core, y * 2 + lax.rem(x, 2))


def shift(v, by, n):
    return lax.rem(v + (by + n), n)


def remote(src, dst, send, recv, where):
    return pltpu.make_async_remote_copy(
        src_ref=src, dst_ref=dst, send_sem=send, recv_sem=recv, device_id=where, device_id_type=MESH
    )


def kernel(
    p_hbm, q_hbm, p_cols, q_cols, out,
    p_in, q_in, held, ids, table, marks, run, part, near, full, zbuf, done, wbuf, ring,
    in_sem, g_send, g_recv, id_send, id_recv, s_send, s_recv, z_send, z_recv, w_send, w_recv, r_send, r_recv,
):
    x, y, z, core = place()
    other = 1 - core
    gather_rings, reduce_rings = (y, x), (x, y)

    def along_y(pos, who):
        return device(x, pos, z, who)

    def along_x(pos, who):
        return device(pos, y, z, who)

    gather_member, reduce_member = (along_y, along_x), (along_x, along_y)
    z_ends = [device(x, y, shift(z, d, 8), core) for d in (1, -1)]
    others = [(by, flip) for by in range(4) for flip in range(2) if by or flip]

    inputs = []
    for f in range(4):
        inputs.append(pltpu.make_async_copy(q_hbm.at[f], q_in.at[f], in_sem.at[f]))
    inputs.append(pltpu.make_async_copy(p_hbm, p_in, in_sem.at[4]))
    for copy in inputs:
        copy.start()

    partners = [along_y(shift(y, by, 4), other if flip else core) for by, flip in others]
    partners += [along_x(shift(x, by, 4), other if flip else core) for by, flip in others if by]
    partners += z_ends
    barrier = pltpu.get_barrier_semaphore()
    for partner in partners:
        pl.semaphore_signal(barrier, inc=1, device_id=partner, device_id_type=MESH)

    started = []

    def launch(copy):
        copy.start()
        started.append(copy)
        return copy

    slot = {0: 0, 1: 2, 3: 4, 2: 6}
    lane = lax.broadcasted_iota(jnp.int32, (8, 128), 1)
    rows = cols = jnp.zeros((8, 128), jnp.int32)
    for f in range(4):
        for k in range(2):
            low = (f * 2 + k) * 6
            rows = jnp.where(jnp.logical_and(lane >= low, lane < low + 6), p_cols[k, f], rows)
        for l in range(6):
            cols = jnp.where(jnp.logical_or(lane == f * 12 + l, lane == f * 12 + 6 + l), q_cols[f, l], cols)
    numbers = jnp.where(lax.broadcasted_iota(jnp.int32, (8, 128), 0) == 0, rows, cols)
    for c in range(2):
        ids[c, 0] = numbers

    def send_numbers():
        for c in range(2):
            for n, (by, flip) in enumerate(others):
                who = gather_member[c](shift(gather_rings[c], by, 4), other if flip else core)
                launch(remote(ids.at[c, 0], ids.at[c, slot[by] + flip], id_send.at[c, n], id_recv.at[c, n], who))

    def stage_block(f):
        inputs[f].wait()
        for c in range(2):
            for k in range(2):
                held[c, 0, f, k * 128 : (k + 1) * 128, :] = p_in[f, k]
        for l in range(6):
            flipped = q_in[f, l].T
            for c in range(2):
                for phase in range(2):
                    low, row = 256 + (phase * 6 + l) * HALF, c * 64 + phase * HALF
                    held[c, 0, f, low : low + HALF, :] = flipped[row : row + HALF]

    def send(phase, c, i, h, source, target, by, flip=False):
        at, rows = pl.ds(h * 2, 2), pl.ds(*BLOCKS[phase])
        who = gather_member[c](shift(gather_rings[c], by, 4), other if flip else core)
        launch(
            remote(
                held.at[c, source, at, rows],
                held.at[c, target, at, rows],
                g_send.at[c, phase, i],
                g_recv.at[c, phase, i],
                who,
            )
        )

    def arrived(phase, c, i, h, target):
        ref = held.at[c, target, pl.ds(h * 2, 2), pl.ds(*BLOCKS[phase])]
        who = gather_member[c](gather_rings[c], other)
        remote(ref, ref, g_send.at[c, phase, i], g_recv.at[c, phase, i], who).wait_recv()

    def send_own(phase):
        for c in range(2):
            send(phase, c, 3, 1, 0, 4, -1)
            send(phase, c, 1, 1, 0, 2, 1)
            send(phase, c, 2, 0, 0, 4, -1)
            send(phase, c, 7, 1, 0, 1, 0, True)

    inputs[4].wait()
    for f in range(2):
        stage_block(f)
    pl.semaphore_wait(barrier, len(partners))
    send_numbers()
    for c in range(2):
        send(0, c, 0, 0, 0, 2, 1)
        send(0, c, 6, 0, 0, 1, 0, True)
    for f in range(2, 4):
        stage_block(f)
    send_own(0)

    for c in range(2):
        for n, (by, flip) in enumerate(others):
            ref = ids.at[c, slot[by] + flip]
            remote(ref, ref, id_send.at[c, n], id_recv.at[c, n], gather_member[c](gather_rings[c], other)).wait_recv()
    below = lax.broadcasted_iota(jnp.int32, (LOAD, 128), 0)
    beside = lax.broadcasted_iota(jnp.int32, (LOAD, 128), 1)
    for c in range(2):
        rows = jnp.concatenate([ids[c, t, 0:1, :] for t in range(8)], axis=0)
        cols = jnp.concatenate([ids[c, t, 1:2, :] for t in range(8)], axis=0)
        mine = jnp.logical_and((rows & 1) == core, lane < LOAD)
        tile_x, tile_z = rows >> 4, (rows >> 1) & 7
        stop_y, stop_x, j = cols >> 3, (cols >> 2) & 1, cols & 3
        if c == 0:
            mine = jnp.logical_and(mine, stop_y == y)
            target = (tile_x * 2 + stop_x) * 32 + tile_z * 4 + j
        else:
            mine = jnp.logical_and(mine, jnp.logical_and(tile_x == lax.div(x, 2), stop_x == lax.rem(x, 2)))
            target = stop_y * 32 + tile_z * 4 + j
        target = jnp.where(mine, target, -1)
        flat = jnp.where(mine, target, -2).T[0:LOAD]
        last = jnp.full((1, 128), -1, jnp.int32)
        for t in range(8):
            same = jnp.broadcast_to(flat[:, t : t + 1], (LOAD, 128)) == beside
            last = jnp.maximum(last, jnp.max(jnp.where(same, below + t * LOAD, -1), axis=0, keepdims=True))
            found = jnp.full((1, 128), -1, jnp.int32)
            mark = jnp.broadcast_to(target[t : t + 1], (LOAD, 128))
            for u in range(t + 1):
                same = jnp.broadcast_to(flat[:, u : u + 1], (LOAD, 128)) == mark
                if u == t:
                    same = jnp.logical_and(same, below < beside)
                found = jnp.maximum(found, jnp.max(jnp.where(same, below + u * LOAD, -1), axis=0, keepdims=True))
            table[c, t : t + 1, :] = jnp.where(found < 0, NONE, found)
        table[c, 8:9, :] = jnp.where(last < 0, NONE, last)
        table[c, 9:16, :] = jnp.zeros((7, 128), jnp.int32)
        run[c, NONE] = jnp.zeros((64, 128), F32)
    copy = pltpu.make_async_copy(table, marks, in_sem.at[5])
    copy.start()
    copy.wait()

    def multiply(phase, c, t):
        low, rows = 256 + phase * 6 * HALF, slice(phase * HALF, (phase + 1) * HALF)

        for f in range(4):
            pair = jnp.concatenate([held[c, t, f, 0:128, :], held[c, t, f, 128:256, :]], axis=1)
            product = jnp.dot(held[c, t, f, low : low + 6 * HALF, :], pair, preferred_element_type=F32)
            for k in range(2):
                sums = []
                for l in range(6):
                    before = run[c, marks[c, t, f * 12 + k * 6 + l], rows]
                    sums.append(product[l * HALF : (l + 1) * HALF, k * 128 : (k + 1) * 128] + before)
                for l in range(6):
                    run[c, t * LOAD + f * 12 + k * 6 + l, rows] = sums[l]

    lent = {1: ((6, 0), (7, 1)), 3: ((8, 0), (9, 1)), 5: ((10, 0), (11, 1)), 7: ((12, 0), (13, 1))}

    def products(phase, t):
        for c in range(2):
            for i, h in lent.get(t, ()):
                arrived(phase, c, i, h, t)
            multiply(phase, c, t)

    def pass_near(phase):
        for c in range(2):
            arrived(phase, c, 0, 0, 2)
            send(phase, c, 4, 0, 2, 6, 1)
            send(phase, c, 8, 0, 2, 3, 0, True)
            arrived(phase, c, 3, 1, 4)
            send(phase, c, 5, 1, 4, 6, -1)
            send(phase, c, 11, 1, 4, 5, 0, True)

    def lend_near(phase):
        for c in range(2):
            arrived(phase, c, 1, 1, 2)
            send(phase, c, 9, 1, 2, 3, 0, True)
            arrived(phase, c, 2, 0, 4)
            send(phase, c, 10, 0, 4, 5, 0, True)

    def lend_far(phase):
        for c in range(2):
            arrived(phase, c, 4, 0, 6)
            send(phase, c, 12, 0, 6, 7, 0, True)
            arrived(phase, c, 5, 1, 6)
            send(phase, c, 13, 1, 6, 7, 0, True)

    products(0, 0)
    products(0, 1)
    pass_near(0)
    for c in range(2):
        send(1, c, 0, 0, 0, 2, 1)
        send(1, c, 6, 0, 0, 1, 0, True)
    send_own(1)
    lend_near(0)
    products(0, 2)
    products(0, 3)
    products(0, 4)
    products(0, 5)
    lend_far(0)
    products(0, 6)
    pass_near(1)
    products(0, 7)

    rings, signs = reduce_rings, (1, -1)
    ends = [[reduce_member[c](shift(rings[c], d, 4), core) for d in signs] for c in range(2)]
    pending = {}

    both = [(c, d) for c in range(2) for d in range(2)]

    def load(start, count):
        rows = slice(start, start + count)
        for c in range(2):

            @pl.loop(0, 8)
            def _(n, c=c):
                for m in range(4):
                    for j in range(4):
                        part[c, m, n, j, rows] = run[c, marks[c, 8, m * 32 + n * 4 + j], rows]

    def send_first(i):
        rows = pl.ds(*CHUNKS[i])
        for c, d in both:
            pending["first", c, d, i] = launch(
                remote(
                    part.at[c, shift(rings[c], 2, 4), pl.ds(4 * d, 4), :, rows],
                    near.at[c, d, :, :, rows],
                    s_send.at[c, d, i, 0],
                    s_recv.at[c, d, i, 0],
                    ends[c][d],
                )
            )

    def send_second(c, d, i, half):
        at, rows = pl.ds(4 * half, 4), pl.ds(*CHUNKS[i])
        n = 2 if half == d else 1
        pending["second", c, d, i, n] = launch(
            remote(
                part.at[c, shift(rings[c], signs[d], 4), at, :, rows],
                full.at[c, d, at, :, rows],
                s_send.at[c, d, i, n],
                s_recv.at[c, d, i, n],
                ends[c][d],
            )
        )

    def send_direct(i):
        for c, d in both:
            send_second(c, d, i, 1 - d)

    def relay(i):
        start, count = CHUNKS[i]
        span = slice(start, start + count)
        for c, d in both:
            pending["first", c, d, i].wait_recv()
            part[c, shift(rings[c], signs[d], 4), 4 * d : 4 * d + 4, :, span] += near[c, d, :, :, span]
            send_second(c, d, i, d)

    def close(i):
        start, count = CHUNKS[i]
        span = slice(start, start + count)
        for c, d in both:
            pending["second", c, d, i, 1].wait_recv()
            pending["second", c, d, i, 2].wait_recv()
        for c in range(2):
            part[c, rings[c], :, :, span] += full[c, 0, :, :, span] + full[c, 1, :, :, span]

    def along_z(i, step):
        start, count = CHUNKS[i]
        for c, d in both:
            target = shift(z, signs[d] * (5 - step), 8)
            low, size = (start + d * count // 2, count // 2) if step < 3 else (start, count)
            if step > 1:
                pending["z", c, d, i, step - 1].wait_recv()
                part[c, rings[c], target, :, low : low + size] += zbuf[c, d, step - 2, :, low : low + size]
            rows = pl.ds(low, size) if step == 1 else pl.ds(start, count)
            pending["z", c, d, i, step] = launch(
                remote(
                    part.at[c, rings[c], target, :, rows],
                    zbuf.at[c, d, step - 1, :, rows],
                    z_send.at[c, d, i, step - 1],
                    z_recv.at[c, d, i, step - 1],
                    z_ends[d],
                )
            )

    def finish(i):
        start, count = CHUNKS[i]
        span = slice(start, start + count)
        for c in range(2):
            for d in range(2):
                pending["z", c, d, i, 4].wait_recv()
            done[:, c * 64 + start : c * 64 + start + count] = (
                part[c, rings[c], z, :, span] + zbuf[c, 0, 3, :, span] + zbuf[c, 1, 3, :, span]
            )

    def wide_z(s, step):
        start, count = WIDE[s]
        for c, d in both:
            target = shift(z, signs[d] * (5 - step), 8)
            low, size = (start + d * count // 2, count // 2) if step < 3 else (start, count)
            if step > 1:
                pending["wide", c, d, s, step - 1].wait_recv()
                part[c, :, target, :, low : low + size] += wbuf[c, d, step - 2, :, :, low : low + size]
            rows = pl.ds(low, size) if step == 1 else pl.ds(start, count)
            pending["wide", c, d, s, step] = launch(
                remote(
                    part.at[c, :, target, :, rows],
                    wbuf.at[c, d, step - 1, :, :, rows],
                    w_send.at[c, d, s, step - 1],
                    w_recv.at[c, d, s, step - 1],
                    z_ends[d],
                )
            )

    def wide_ring(s):
        start, count = WIDE[s]
        span = slice(start, start + count)
        for c in range(2):
            for d in range(2):
                pending["wide", c, d, s, 4].wait_recv()
            part[c, :, z, :, span] += wbuf[c, 0, 3, :, :, span] + wbuf[c, 1, 3, :, :, span]
            for d in range(2):
                half = pl.ds(start + d * count // 2, count // 2)
                pending["half", c, d, s] = launch(
                    remote(
                        part.at[c, shift(rings[c], 2, 4), z, :, half],
                        ring.at[0, c, d, :, half],
                        r_send.at[c, d, s, 0],
                        r_recv.at[c, d, s, 0],
                        ends[c][d],
                    )
                )

    def wide_relay(s):
        start, count = WIDE[s]
        rows = pl.ds(start, count)
        for c, d in both:
            pending["half", c, d, s].wait_recv()
            low, spot = start + d * count // 2, shift(rings[c], signs[d], 4)
            half = slice(low, low + count // 2)
            part[c, spot, z, :, half] += ring[0, c, d, :, half]
            pending["whole", c, d, s] = launch(
                remote(
                    part.at[c, spot, z, :, rows],
                    ring.at[1, c, d, :, rows],
                    r_send.at[c, d, s, 1],
                    r_recv.at[c, d, s, 1],
                    ends[c][d],
                )
            )

    def wide_finish(s):
        start, count = WIDE[s]
        span = slice(start, start + count)
        for c in range(2):
            for d in range(2):
                pending["whole", c, d, s].wait_recv()
            done[:, c * 64 + start : c * 64 + start + count] = (
                part[c, rings[c], z, :, span] + ring[1, c, 0, :, span] + ring[1, c, 1, :, span]
            )

    steps = {
        "load": lambda i: load(*CHUNKS[i]), "first": send_first, "direct": send_direct, "relay": relay,
        "close": close, "z": along_z, "finish": finish, "wload": lambda i: load(*WIDE[i]), "wz": wide_z,
        "wring": wide_ring, "wrelay": wide_relay, "wfinish": wide_finish, "mul": lambda t: products(1, t),
        "near": lambda i: lend_near(1), "far": lambda i: lend_far(1),
    }
    for step in ORDER:
        steps[step[0]](*step[1:])
    for j in range(4):
        out[:, j * 128 : (j + 1) * 128] = done[j].T
    for copy in started:
        copy.wait_send()


def body(p_tiles, p_cols, q_tiles, q_cols):
    dma = pltpu.SemaphoreType.DMA
    return pl.pallas_call(
        kernel,
        name="coarse",
        out_shape=jax.ShapeDtypeStruct((128, 512), F32),
        in_specs=[ANY, ANY, SMEM, SMEM],
        out_specs=VMEM,
        scratch_shapes=[
            pltpu.VMEM((4, 2, 128, 128), BF16),
            pltpu.VMEM((4, 6, 128, 128), BF16),
            pltpu.VMEM((2, 8, 4, RECORD, 128), BF16),
            pltpu.VMEM((2, 8, 8, 128), jnp.int32),
            pltpu.VMEM((2, 16, 128), jnp.int32),
            pltpu.SMEM((2, 16, 128), jnp.int32),
            pltpu.VMEM((2, NONE + 1, 64, 128), F32),
            pltpu.VMEM((2, 4, 8, 4, 64, 128), F32),
            pltpu.VMEM((2, 2, 4, 4, 64, 128), F32),
            pltpu.VMEM((2, 2, 8, 4, 64, 128), F32),
            pltpu.VMEM((2, 2, 4, 4, 64, 128), F32),
            pltpu.VMEM((4, 128, 128), F32),
            pltpu.VMEM((2, 2, 4, 4, 4, HALF, 128), F32),
            pltpu.VMEM((2, 2, 2, 4, HALF, 128), F32),
            dma((6,)),
            dma((2, 2, 14)),
            dma((2, 2, 14)),
            dma((2, 7)),
            dma((2, 7)),
            dma((2, 2, len(CHUNKS), 3)),
            dma((2, 2, len(CHUNKS), 3)),
            dma((2, 2, len(CHUNKS), 4)),
            dma((2, 2, len(CHUNKS), 4)),
            dma((2, 2, len(WIDE), 4)),
            dma((2, 2, len(WIDE), 4)),
            dma((2, 2, len(WIDE), 2)),
            dma((2, 2, len(WIDE), 2)),
        ],
        compiler_params=pltpu.CompilerParams(
            collective_id=0, has_side_effects=True, vmem_limit_bytes=60 << 20
        ),
    )(p_tiles, q_tiles, p_cols.T, q_cols)


def solution(mesh):
    placed = (
        P(("row", "col"), None, None, None),
        P(("row", "col"), None),
        P(("row", "col"), None, None, None),
        P(("row", "col"), None),
    )
    return jax.shard_map(
        body, mesh=mesh, in_specs=placed, out_specs=P("row", "col"), check_vma=False
    )
```

```python
import jax
import jax.numpy as jnp
from jax import lax
from jax.experimental import pallas as pl
from jax.experimental.pallas import tpu as pltpu
from jax.sharding import PartitionSpec as P

MESH = pl.DeviceIdType.MESH
BF16, F32 = jnp.bfloat16, jnp.float32
ANY = pl.BlockSpec(memory_space=pl.ANY)
VMEM = pl.BlockSpec(memory_space=pltpu.VMEM)
SMEM = pl.BlockSpec(memory_space=pltpu.SMEM)
RECORD = 640
LOAD = 48
NONE = 8 * LOAD
HALF = 32
BLOCKS = ((0, 256 + 6 * HALF), (256 + 6 * HALF, 6 * HALF))
CHUNKS = ((16, 16), (32, 16), (48, 16))
WIDE = ((0, 16),)
ORDER = (
    ("wload", 0), ("wz", 0, 1), ("mul", 0), ("load", 0), ("near", 0), ("first", 0), ("mul", 1), ("mul", 2),
    ("direct", 0), ("wz", 0, 2), ("mul", 3), ("mul", 4), ("far", 0), ("mul", 5), ("relay", 0), ("mul", 6),
    ("mul", 7), ("load", 1), ("first", 1), ("load", 2), ("direct", 1), ("wz", 0, 3), ("relay", 1), ("close", 0),
    ("first", 2), ("z", 0, 1), ("wz", 0, 4), ("direct", 2), ("z", 0, 2), ("close", 1), ("relay", 2), ("z", 1, 1),
    ("z", 0, 3), ("z", 1, 2), ("wring", 0), ("close", 2), ("z", 2, 1), ("z", 1, 3), ("z", 2, 2), ("z", 1, 4),
    ("z", 2, 3), ("z", 0, 4), ("wrelay", 0), ("finish", 1), ("z", 2, 4), ("finish", 0), ("wfinish", 0),
    ("finish", 2),
)


def place():
    row, col = lax.axis_index("row"), lax.axis_index("col")
    core, z = lax.rem(row, 2), lax.rem(lax.div(row, 2), 8)
    x = lax.div(row, 16) * 2 + lax.rem(col, 2)
    return x, lax.div(col, 2), z, core


def device(x, y, z, core):
    return (lax.div(x, 2) * 16 + z * 2 + core, y * 2 + lax.rem(x, 2))


def shift(v, by, n):
    return lax.rem(v + (by + n), n)


def remote(src, dst, send, recv, where):
    return pltpu.make_async_remote_copy(
        src_ref=src, dst_ref=dst, send_sem=send, recv_sem=recv, device_id=where, device_id_type=MESH
    )


def kernel(
    p_hbm, q_hbm, p_cols, q_cols, out,
    p_in, q_in, held, ids, table, marks, run, part, near, full, zbuf, done, wbuf, ring,
    in_sem, g_send, g_recv, id_send, id_recv, s_send, s_recv, z_send, z_recv, w_send, w_recv, r_send, r_recv,
):
    x, y, z, core = place()
    other = 1 - core
    gather_rings, reduce_rings = (y, x), (x, y)

    def along_y(pos, who):
        return device(x, pos, z, who)

    def along_x(pos, who):
        return device(pos, y, z, who)

    gather_member, reduce_member = (along_y, along_x), (along_x, along_y)
    z_ends = [device(x, y, shift(z, d, 8), core) for d in (1, -1)]
    others = [(by, flip) for by in range(4) for flip in range(2) if by or flip]

    inputs = []
    for f in range(4):
        inputs.append(pltpu.make_async_copy(q_hbm.at[f], q_in.at[f], in_sem.at[f]))
    inputs.append(pltpu.make_async_copy(p_hbm, p_in, in_sem.at[4]))
    for copy in inputs:
        copy.start()

    partners = [along_y(shift(y, by, 4), other if flip else core) for by, flip in others]
    partners += [along_x(shift(x, by, 4), other if flip else core) for by, flip in others if by]
    partners += z_ends
    barrier = pltpu.get_barrier_semaphore()
    for partner in partners:
        pl.semaphore_signal(barrier, inc=1, device_id=partner, device_id_type=MESH)

    started = []

    def launch(copy):
        copy.start()
        started.append(copy)
        return copy

    slot = {0: 0, 1: 2, 3: 4, 2: 6}
    lane = lax.broadcasted_iota(jnp.int32, (8, 128), 1)
    rows = cols = jnp.zeros((8, 128), jnp.int32)
    for f in range(4):
        for k in range(2):
            low = (f * 2 + k) * 6
            rows = jnp.where(jnp.logical_and(lane >= low, lane < low + 6), p_cols[k, f], rows)
        for l in range(6):
            cols = jnp.where(jnp.logical_or(lane == f * 12 + l, lane == f * 12 + 6 + l), q_cols[f, l], cols)
    numbers = jnp.where(lax.broadcasted_iota(jnp.int32, (8, 128), 0) == 0, rows, cols)
    for c in range(2):
        ids[c, 0] = numbers

    def send_numbers():
        for c in range(2):
            for n, (by, flip) in enumerate(others):
                who = gather_member[c](shift(gather_rings[c], by, 4), other if flip else core)
                launch(remote(ids.at[c, 0], ids.at[c, slot[by] + flip], id_send.at[c, n], id_recv.at[c, n], who))

    def stage_block(f):
        inputs[f].wait()
        for c in range(2):
            for k in range(2):
                held[c, 0, f, k * 128 : (k + 1) * 128, :] = p_in[f, k]
        for l in range(6):
            flipped = q_in[f, l].T
            for c in range(2):
                for phase in range(2):
                    low, row = 256 + (phase * 6 + l) * HALF, c * 64 + phase * HALF
                    held[c, 0, f, low : low + HALF, :] = flipped[row : row + HALF]

    def send(phase, c, i, h, source, target, by, flip=False):
        at, rows = pl.ds(h * 2, 2), pl.ds(*BLOCKS[phase])
        who = gather_member[c](shift(gather_rings[c], by, 4), other if flip else core)
        launch(
            remote(
                held.at[c, source, at, rows],
                held.at[c, target, at, rows],
                g_send.at[c, phase, i],
                g_recv.at[c, phase, i],
                who,
            )
        )

    def arrived(phase, c, i, h, target):
        ref = held.at[c, target, pl.ds(h * 2, 2), pl.ds(*BLOCKS[phase])]
        who = gather_member[c](gather_rings[c], other)
        remote(ref, ref, g_send.at[c, phase, i], g_recv.at[c, phase, i], who).wait_recv()

    def send_own(phase):
        for c in range(2):
            send(phase, c, 3, 1, 0, 4, -1)
            send(phase, c, 1, 1, 0, 2, 1)
            send(phase, c, 2, 0, 0, 4, -1)
            send(phase, c, 7, 1, 0, 1, 0, True)

    inputs[4].wait()
    for f in range(2):
        stage_block(f)
    pl.semaphore_wait(barrier, len(partners))
    send_numbers()
    for c in range(2):
        send(0, c, 0, 0, 0, 2, 1)
        send(0, c, 6, 0, 0, 1, 0, True)
    for f in range(2, 4):
        stage_block(f)
    send_own(0)

    for c in range(2):
        for n, (by, flip) in enumerate(others):
            ref = ids.at[c, slot[by] + flip]
            remote(ref, ref, id_send.at[c, n], id_recv.at[c, n], gather_member[c](gather_rings[c], other)).wait_recv()
    below = lax.broadcasted_iota(jnp.int32, (LOAD, 128), 0)
    beside = lax.broadcasted_iota(jnp.int32, (LOAD, 128), 1)
    for c in range(2):
        rows = jnp.concatenate([ids[c, t, 0:1, :] for t in range(8)], axis=0)
        cols = jnp.concatenate([ids[c, t, 1:2, :] for t in range(8)], axis=0)
        mine = jnp.logical_and((rows & 1) == core, lane < LOAD)
        tile_x, tile_z = rows >> 4, (rows >> 1) & 7
        stop_y, stop_x, j = cols >> 3, (cols >> 2) & 1, cols & 3
        if c == 0:
            mine = jnp.logical_and(mine, stop_y == y)
            target = (tile_x * 2 + stop_x) * 32 + tile_z * 4 + j
        else:
            mine = jnp.logical_and(mine, jnp.logical_and(tile_x == lax.div(x, 2), stop_x == lax.rem(x, 2)))
            target = stop_y * 32 + tile_z * 4 + j
        target = jnp.where(mine, target, -1)
        flat = jnp.where(mine, target, -2).T[0:LOAD]
        last = jnp.full((1, 128), -1, jnp.int32)
        for t in range(8):
            same = jnp.broadcast_to(flat[:, t : t + 1], (LOAD, 128)) == beside
            last = jnp.maximum(last, jnp.max(jnp.where(same, below + t * LOAD, -1), axis=0, keepdims=True))
            found = jnp.full((1, 128), -1, jnp.int32)
            mark = jnp.broadcast_to(target[t : t + 1], (LOAD, 128))
            for u in range(t + 1):
                same = jnp.broadcast_to(flat[:, u : u + 1], (LOAD, 128)) == mark
                if u == t:
                    same = jnp.logical_and(same, below < beside)
                found = jnp.maximum(found, jnp.max(jnp.where(same, below + u * LOAD, -1), axis=0, keepdims=True))
            table[c, t : t + 1, :] = jnp.where(found < 0, NONE, found)
        table[c, 8:9, :] = jnp.where(last < 0, NONE, last)
        table[c, 9:16, :] = jnp.zeros((7, 128), jnp.int32)
        run[c, NONE] = jnp.zeros((64, 128), F32)
    copy = pltpu.make_async_copy(table, marks, in_sem.at[5])
    copy.start()
    copy.wait()

    def multiply(phase, c, t):
        low, rows = 256 + phase * 6 * HALF, slice(phase * HALF, (phase + 1) * HALF)

        for f in range(4):
            pair = jnp.concatenate([held[c, t, f, 0:128, :], held[c, t, f, 128:256, :]], axis=1)
            product = jnp.dot(held[c, t, f, low : low + 6 * HALF, :], pair, preferred_element_type=F32)
            for k in range(2):
                sums = []
                for l in range(6):
                    before = run[c, marks[c, t, f * 12 + k * 6 + l], rows]
                    sums.append(product[l * HALF : (l + 1) * HALF, k * 128 : (k + 1) * 128] + before)
                for l in range(6):
                    run[c, t * LOAD + f * 12 + k * 6 + l, rows] = sums[l]

    lent = {1: ((6, 0), (7, 1)), 3: ((8, 0), (9, 1)), 5: ((10, 0), (11, 1)), 7: ((12, 0), (13, 1))}

    def products(phase, t):
        for c in range(2):
            for i, h in lent.get(t, ()):
                arrived(phase, c, i, h, t)
            multiply(phase, c, t)

    def pass_near(phase):
        for c in range(2):
            arrived(phase, c, 0, 0, 2)
            send(phase, c, 4, 0, 2, 6, 1)
            send(phase, c, 8, 0, 2, 3, 0, True)
            arrived(phase, c, 3, 1, 4)
            send(phase, c, 5, 1, 4, 6, -1)
            send(phase, c, 11, 1, 4, 5, 0, True)

    def lend_near(phase):
        for c in range(2):
            arrived(phase, c, 1, 1, 2)
            send(phase, c, 9, 1, 2, 3, 0, True)
            arrived(phase, c, 2, 0, 4)
            send(phase, c, 10, 0, 4, 5, 0, True)

    def lend_far(phase):
        for c in range(2):
            arrived(phase, c, 4, 0, 6)
            send(phase, c, 12, 0, 6, 7, 0, True)
            arrived(phase, c, 5, 1, 6)
            send(phase, c, 13, 1, 6, 7, 0, True)

    products(0, 0)
    products(0, 1)
    pass_near(0)
    for c in range(2):
        send(1, c, 0, 0, 0, 2, 1)
        send(1, c, 6, 0, 0, 1, 0, True)
    send_own(1)
    lend_near(0)
    products(0, 2)
    products(0, 3)
    products(0, 4)
    products(0, 5)
    lend_far(0)
    products(0, 6)
    pass_near(1)
    products(0, 7)

    rings, signs = reduce_rings, (1, -1)
    ends = [[reduce_member[c](shift(rings[c], d, 4), core) for d in signs] for c in range(2)]
    pending = {}

    both = [(c, d) for c in range(2) for d in range(2)]

    def load(start, count):
        rows = slice(start, start + count)
        for c in range(2):
            for m in range(4):
                for n in range(8):
                    for j in range(4):
                        part[c, m, n, j, rows] = run[c, marks[c, 8, m * 32 + n * 4 + j], rows]

    def send_first(i):
        rows = pl.ds(*CHUNKS[i])
        for c, d in both:
            pending["first", c, d, i] = launch(
                remote(
                    part.at[c, shift(rings[c], 2, 4), pl.ds(4 * d, 4), :, rows],
                    near.at[c, d, :, :, rows],
                    s_send.at[c, d, i, 0],
                    s_recv.at[c, d, i, 0],
                    ends[c][d],
                )
            )

    def send_second(c, d, i, half):
        at, rows = pl.ds(4 * half, 4), pl.ds(*CHUNKS[i])
        n = 2 if half == d else 1
        pending["second", c, d, i, n] = launch(
            remote(
                part.at[c, shift(rings[c], signs[d], 4), at, :, rows],
                full.at[c, d, at, :, rows],
                s_send.at[c, d, i, n],
                s_recv.at[c, d, i, n],
                ends[c][d],
            )
        )

    def send_direct(i):
        for c, d in both:
            send_second(c, d, i, 1 - d)

    def relay(i):
        start, count = CHUNKS[i]
        span = slice(start, start + count)
        for c, d in both:
            pending["first", c, d, i].wait_recv()
            part[c, shift(rings[c], signs[d], 4), 4 * d : 4 * d + 4, :, span] += near[c, d, :, :, span]
            send_second(c, d, i, d)

    def close(i):
        start, count = CHUNKS[i]
        span = slice(start, start + count)
        for c, d in both:
            pending["second", c, d, i, 1].wait_recv()
            pending["second", c, d, i, 2].wait_recv()
        for c in range(2):
            part[c, rings[c], :, :, span] += full[c, 0, :, :, span] + full[c, 1, :, :, span]

    def along_z(i, step):
        start, count = CHUNKS[i]
        for c, d in both:
            target = shift(z, signs[d] * (5 - step), 8)
            low, size = (start + d * count // 2, count // 2) if step < 3 else (start, count)
            if step > 1:
                pending["z", c, d, i, step - 1].wait_recv()
                part[c, rings[c], target, :, low : low + size] += zbuf[c, d, step - 2, :, low : low + size]
            rows = pl.ds(low, size) if step == 1 else pl.ds(start, count)
            pending["z", c, d, i, step] = launch(
                remote(
                    part.at[c, rings[c], target, :, rows],
                    zbuf.at[c, d, step - 1, :, rows],
                    z_send.at[c, d, i, step - 1],
                    z_recv.at[c, d, i, step - 1],
                    z_ends[d],
                )
            )

    def finish(i):
        start, count = CHUNKS[i]
        span = slice(start, start + count)
        for c in range(2):
            for d in range(2):
                pending["z", c, d, i, 4].wait_recv()
            done[:, c * 64 + start : c * 64 + start + count] = (
                part[c, rings[c], z, :, span] + zbuf[c, 0, 3, :, span] + zbuf[c, 1, 3, :, span]
            )

    def wide_z(s, step):
        start, count = WIDE[s]
        for c, d in both:
            target = shift(z, signs[d] * (5 - step), 8)
            low, size = (start + d * count // 2, count // 2) if step < 3 else (start, count)
            if step > 1:
                pending["wide", c, d, s, step - 1].wait_recv()
                part[c, :, target, :, low : low + size] += wbuf[c, d, step - 2, :, :, low : low + size]
            rows = pl.ds(low, size) if step == 1 else pl.ds(start, count)
            pending["wide", c, d, s, step] = launch(
                remote(
                    part.at[c, :, target, :, rows],
                    wbuf.at[c, d, step - 1, :, :, rows],
                    w_send.at[c, d, s, step - 1],
                    w_recv.at[c, d, s, step - 1],
                    z_ends[d],
                )
            )

    def wide_ring(s):
        start, count = WIDE[s]
        span = slice(start, start + count)
        for c in range(2):
            for d in range(2):
                pending["wide", c, d, s, 4].wait_recv()
            part[c, :, z, :, span] += wbuf[c, 0, 3, :, :, span] + wbuf[c, 1, 3, :, :, span]
            for d in range(2):
                half = pl.ds(start + d * count // 2, count // 2)
                pending["half", c, d, s] = launch(
                    remote(
                        part.at[c, shift(rings[c], 2, 4), z, :, half],
                        ring.at[0, c, d, :, half],
                        r_send.at[c, d, s, 0],
                        r_recv.at[c, d, s, 0],
                        ends[c][d],
                    )
                )

    def wide_relay(s):
        start, count = WIDE[s]
        rows = pl.ds(start, count)
        for c, d in both:
            pending["half", c, d, s].wait_recv()
            low, spot = start + d * count // 2, shift(rings[c], signs[d], 4)
            half = slice(low, low + count // 2)
            part[c, spot, z, :, half] += ring[0, c, d, :, half]
            pending["whole", c, d, s] = launch(
                remote(
                    part.at[c, spot, z, :, rows],
                    ring.at[1, c, d, :, rows],
                    r_send.at[c, d, s, 1],
                    r_recv.at[c, d, s, 1],
                    ends[c][d],
                )
            )

    def wide_finish(s):
        start, count = WIDE[s]
        span = slice(start, start + count)
        for c in range(2):
            for d in range(2):
                pending["whole", c, d, s].wait_recv()
            done[:, c * 64 + start : c * 64 + start + count] = (
                part[c, rings[c], z, :, span] + ring[1, c, 0, :, span] + ring[1, c, 1, :, span]
            )

    steps = {
        "load": lambda i: load(*CHUNKS[i]), "first": send_first, "direct": send_direct, "relay": relay,
        "close": close, "z": along_z, "finish": finish, "wload": lambda i: load(*WIDE[i]), "wz": wide_z,
        "wring": wide_ring, "wrelay": wide_relay, "wfinish": wide_finish, "mul": lambda t: products(1, t),
        "near": lambda i: lend_near(1), "far": lambda i: lend_far(1),
    }
    for step in ORDER:
        steps[step[0]](*step[1:])
    for j in range(4):
        out[:, j * 128 : (j + 1) * 128] = done[j].T
    for copy in started:
        copy.wait_send()


def body(p_tiles, p_cols, q_tiles, q_cols):
    dma = pltpu.SemaphoreType.DMA
    return pl.pallas_call(
        kernel,
        name="coarse",
        out_shape=jax.ShapeDtypeStruct((128, 512), F32),
        in_specs=[ANY, ANY, SMEM, SMEM],
        out_specs=VMEM,
        scratch_shapes=[
            pltpu.VMEM((4, 2, 128, 128), BF16),
            pltpu.VMEM((4, 6, 128, 128), BF16),
            pltpu.VMEM((2, 8, 4, RECORD, 128), BF16),
            pltpu.VMEM((2, 8, 8, 128), jnp.int32),
            pltpu.VMEM((2, 16, 128), jnp.int32),
            pltpu.SMEM((2, 16, 128), jnp.int32),
            pltpu.VMEM((2, NONE + 1, 64, 128), F32),
            pltpu.VMEM((2, 4, 8, 4, 64, 128), F32),
            pltpu.VMEM((2, 2, 4, 4, 64, 128), F32),
            pltpu.VMEM((2, 2, 8, 4, 64, 128), F32),
            pltpu.VMEM((2, 2, 4, 4, 64, 128), F32),
            pltpu.VMEM((4, 128, 128), F32),
            pltpu.VMEM((2, 2, 4, 4, 4, HALF, 128), F32),
            pltpu.VMEM((2, 2, 2, 4, HALF, 128), F32),
            dma((6,)),
            dma((2, 2, 14)),
            dma((2, 2, 14)),
            dma((2, 7)),
            dma((2, 7)),
            dma((2, 2, len(CHUNKS), 3)),
            dma((2, 2, len(CHUNKS), 3)),
            dma((2, 2, len(CHUNKS), 4)),
            dma((2, 2, len(CHUNKS), 4)),
            dma((2, 2, len(WIDE), 4)),
            dma((2, 2, len(WIDE), 4)),
            dma((2, 2, len(WIDE), 2)),
            dma((2, 2, len(WIDE), 2)),
        ],
        compiler_params=pltpu.CompilerParams(
            collective_id=0, has_side_effects=True, vmem_limit_bytes=60 << 20
        ),
    )(p_tiles, q_tiles, p_cols.T, q_cols)


def solution(mesh):
    placed = (
        P(("row", "col"), None, None, None),
        P(("row", "col"), None),
        P(("row", "col"), None, None, None),
        P(("row", "col"), None),
    )
    return jax.shard_map(
        body, mesh=mesh, in_specs=placed, out_specs=P("row", "col"), check_vma=False
    )
```
